256 devices in a mesh: tensor: 8 (over z), expert: 32 (over x, y, core).
Axes of the slice: x: 4, y: 4, z: 8, core: 2. Of those that a mesh axis runs over, the one named last changes fastest.
Arguments:
- queries: bfloat16 [2048, 64, 576], P('expert', 'tensor'), may hold values from -50 to 50
- latent_cache: bfloat16 [32768, 576], P('expert'), may hold values from -5 to 5
- new_latents: bfloat16 [2048, 576], P('expert'), may hold values from -5 to 5
- residual: bfloat16 [2048, 3584], P(('expert', 'tensor')), may hold values from -6 to 6
- w_uv: bfloat16 [32768, 128], P(('tensor', 'expert')), may hold values from -0.25 to 0.25
- w_out: bfloat16 [8192, 3584], P(('tensor', 'expert')), may hold values from -0.0625 to 0.0625
- norm_gain: float32 [3584], replicated, may hold values from 0.25 to 1.75
- expert_ids: int32 [2048, 8], P('expert'), may hold values from 0 to 127, all different within a row; in each aligned block of 64 rows (0 to 63, 64 to 127, ...) at most 8 rows name the same one
- gate_weights: float32 [2048, 8], P('expert'), may hold values from 0.1 to 0.6
- w_gate: bfloat16 [128, 3584, 1024], P('expert', None, 'tensor'), may hold values from -0.09375 to 0.09375
- w_up: bfloat16 [128, 3584, 1024], P('expert', None, 'tensor'), may hold values from -0.09375 to 0.09375
- w_down: bfloat16 [128, 1024, 3584], P('expert', 'tensor'), may hold values from -0.1875 to 0.1875
Outputs:
- layer_out: bfloat16 [2048, 3584], P(('expert', 'tensor'))
The draws below stay inside these ranges and needn't reach their ends.
Inputs may be any that keep to these rules, and one draw needn't show every extreme that they name: `expert_ids`: within each token group of 64 tokens no expert is chosen by more than 8 routes, some expert by exactly 8; a token names 8 different experts.
All inputs are finite; a program needn't handle non-finite values.
Results may differ from the reference program's by a relative error of at most 0.01.
Values may be sent and summed in bfloat16 or wider, within the bound.
No kernel may reach another device: no remote copies, remote signals or barrier semaphores. Data moves between devices by JAX's collectives and lax.ppermute only.
A program may use at most 128 MiB of HBM per device.

```python
import math
import jax
import jax.numpy as jnp
import numpy as np
from jax import lax

D = 3584
HEADS = 64
LATENT = 512
ROPE = 64
VDIM = 128
QDIM = 576
FF = 1024
EXPERTS = 128
TOP = 8
TOK_GRP = 64
CTX = 1024
CAP = 8
TOKENS = 2048
N_TENSOR = 8
N_EXPERT = 32


def draw_latent_cache(key, part):
    values_all = jnp.clip(jax.random.normal(jax.random.fold_in(key, 3), (N_EXPERT, CTX, QDIM), jnp.float32), -5.0, 5.0)
    return values_all.reshape(N_EXPERT * CTX, QDIM).astype(jnp.bfloat16)


def draw_queries(key, part):
    values_all = jnp.clip(jax.random.normal(jax.random.fold_in(key, 5), (N_EXPERT, TOK_GRP, HEADS, QDIM), jnp.float32), -5.0, 5.0)
    return values_all.reshape(TOKENS, HEADS, QDIM).astype(jnp.bfloat16)


def steps_of(rng, shape, shards, low, top_value):
    factor_of = 1.0
    for dim, shards_of in shards:
        draws = jax.random.uniform(jax.random.fold_in(jax.random.fold_in(rng, 6), dim), (shards_of,), jnp.float32, low / len(shards), top_value / len(shards))
        factor_of = factor_of * jnp.repeat(jnp.exp(draws), shape[dim] // shards_of).reshape((-1,) + (1,) * (len(shape) - 1 - dim))
    return factor_of


def shared_out(key, own, number, rows, number_of, top, limit, slope):
    sequence = jax.random.permutation(key, number_of)
    crowded, common = portions_of(number_of, rows * top, limit, slope, True), portions_of(number_of, rows * top, limit, slope, False)
    places = jnp.arange(number_of)

    def named(tallies, turn):
        used = int((tallies > 0).sum())
        fixed = max(1, used // 4)
        shifted = fixed + (places - fixed + turn * (used - fixed)) % max(1, number_of - fixed)
        return jnp.zeros((number_of,), jnp.int32).at[sequence[jnp.where(places < fixed, places, shifted)]].set(jnp.asarray(tallies, jnp.int32))

    tallies = jnp.where(number % 4 == 0, named(crowded, number // 4), named(common, number - number // 4 - 1))
    mixed = jax.random.permutation(jax.random.fold_in(own, 3), number_of)
    giver, taker = mixed[0:number_of // 2 * 2:2], mixed[1:number_of // 2 * 2:2]
    slack = jnp.minimum(tallies[giver] - 1, limit - tallies[taker]) // 2
    slack = jnp.where((giver == sequence[0]) | (taker == sequence[0]) | (tallies[taker] == 0), 0, jnp.maximum(slack, 0))
    shifted = jax.random.randint(jax.random.fold_in(own, 4), (number_of // 2,), 0, 1 << 20) % (slack + 1)
    tallies = tallies.at[giver].add(-shifted).at[taker].add(shifted)
    items = jnp.searchsorted(jnp.cumsum(tallies), jnp.arange(rows * top), side="right").astype(jnp.int32)
    listing = items.reshape(top, rows).T
    listing = listing[jax.random.permutation(jax.random.fold_in(own, 1), rows)]
    turn = jax.random.randint(jax.random.fold_in(own, 2), (rows, 1), 0, top)
    return jnp.take_along_axis(listing, (jnp.arange(top)[None, :] + turn) % top, axis=1)


def portions_of(amount, total, bound, lean, full):
    loads = [(1 << 20) // math.isqrt(rank ** lean) + 1 for rank in range(1, amount + 1)]
    largest = bound if full else min(bound, max(-(-total // amount), total * loads[0] // sum(loads)))
    least = 1 if total - largest >= amount - 1 else 0
    holding, rest = [largest] + [least] * (amount - 1), total - largest - least * (amount - 1)
    while rest > 0:
        free = [i for i in range(1, amount) if holding[i] < largest] or [i for i in range(1, amount) if holding[i] < bound]
        pool, budget = sum([loads[i] for i in free]), rest
        for i in free:
            extra = min(bound - holding[i], max(1, budget * loads[i] // pool), rest)
            holding[i] = holding[i] + extra
            rest = rest - extra
    return np.array(holding)


def gaussian(own_key, extent, scale, most, cuts=(), held_as=jnp.bfloat16):
    array = scale * jax.random.normal(own_key, extent, jnp.float32)
    if cuts:
        array = array * steps_of(own_key, extent, cuts, -0.22, 0.18)
    return jnp.clip(array, -most, most).astype(held_as)


def setup_inputs(seed: int = 0) -> dict:
    streams_of = jax.random.split(jax.random.key(seed), 13)
    queries = draw_queries(jax.random.fold_in(streams_of[12], 71), 0)
    latent_cache = draw_latent_cache(jax.random.fold_in(streams_of[12], 71), 0)
    new_latents = gaussian(streams_of[2], (TOKENS, QDIM), 1.0, 5.0, ((0, 32),))
    residual = gaussian(streams_of[3], (TOKENS, D), 1.0, 6.0, ((0, 256),))
    w_uv = gaussian(streams_of[4], (HEADS * LATENT, VDIM), LATENT ** -0.5, 0.25, ((0, 256),))
    w_out = gaussian(streams_of[5], (HEADS * VDIM, D), (HEADS * VDIM) ** -0.5, 0.0625, ((0, 256),))
    norm_gain = jnp.clip(1.0 + 0.15 * jax.random.normal(streams_of[6], (D,), jnp.float32), 0.25, 1.75)
    expert_ids_keys = jax.random.split(jax.random.fold_in(streams_of[7], 1), TOKENS // TOK_GRP)
    expert_ids_turns = jax.random.permutation(jax.random.fold_in(streams_of[7], 3), TOKENS // TOK_GRP)
    expert_ids = jax.vmap(lambda own, number: shared_out(jax.random.fold_in(streams_of[7], 2), own, number, TOK_GRP, EXPERTS, TOP, CAP, 2))(expert_ids_keys, expert_ids_turns).reshape((TOKENS, TOP))
    gate_weights = jnp.clip(0.1 + 0.5 * jax.random.uniform(streams_of[8], (TOKENS, TOP), jnp.float32) ** steps_of(streams_of[8], (TOKENS, TOP), ((0, 32),), -0.2, 0.2), 0.1, 0.6)
    w_gate = gaussian(streams_of[9], (EXPERTS, D, FF), D ** -0.5, 0.09375, ((0, 32), (2, 8)))
    w_up = gaussian(streams_of[10], (EXPERTS, D, FF), D ** -0.5, 0.09375, ((0, 32), (2, 8)))
    w_down = gaussian(streams_of[11], (EXPERTS, FF, D), FF ** -0.5, 0.1875, ((0, 32), (1, 8)))
    return dict(queries=queries, latent_cache=latent_cache, new_latents=new_latents, residual=residual, w_uv=w_uv, w_out=w_out, norm_gain=norm_gain, expert_ids=expert_ids, gate_weights=gate_weights, w_gate=w_gate, w_up=w_up, w_down=w_down)


EPSILON = 1e-06

def route_slots(route_ids):
    onehot = (route_ids[:, None] == jnp.arange(EXPERTS, dtype=jnp.int32)[None, :]).astype(jnp.int32)
    before = jnp.cumsum(onehot, axis=0) - onehot
    return lax.optimization_barrier(jnp.sum(before * onehot, axis=1)).astype(jnp.int32)

def reference(queries, latent_cache, new_latents, residual, w_uv, w_out, norm_gain, expert_ids, gate_weights, w_gate, w_up, w_down):
    uv_heads = w_uv.reshape(HEADS, LATENT, VDIM).astype(jnp.float32)
    score_scale = (VDIM + ROPE) ** (-0.5)

    def attend_group(inputs):
        group_q, group_cache, group_new = inputs
        key_rows = jnp.concatenate([group_cache, group_new], axis=0)
        scores = jnp.einsum('thc,kc->htk', group_q.astype(jnp.float32), key_rows.astype(jnp.float32)) * score_scale
        query_pos = jnp.arange(TOK_GRP, dtype=jnp.int32)[:, None]
        key_pos = jnp.arange(CTX + TOK_GRP, dtype=jnp.int32)[None, :] - CTX
        scores = jnp.where((key_pos <= query_pos)[None], scores, -jnp.inf)
        row_peak = lax.optimization_barrier(jnp.max(scores, axis=2, keepdims=True))
        exp_scores = jnp.exp(scores - row_peak)
        attn_probs = (exp_scores / lax.optimization_barrier(jnp.sum(exp_scores, axis=2, keepdims=True))).astype(jnp.bfloat16)
        attended = jnp.einsum('htk,kl->thl', attn_probs.astype(jnp.float32), key_rows[:, :LATENT].astype(jnp.float32)).astype(jnp.bfloat16)
        head_values = jnp.einsum('thl,hlv->thv', attended.astype(jnp.float32), uv_heads).astype(jnp.bfloat16)
        return head_values
    head_values = lax.map(attend_group, (queries.reshape(N_EXPERT, TOK_GRP, HEADS, QDIM), latent_cache.reshape(N_EXPERT, CTX, QDIM), new_latents.reshape(N_EXPERT, TOK_GRP, QDIM)))
    attn_out = jnp.dot(head_values.reshape(TOKENS, HEADS * VDIM), w_out, preferred_element_type=jnp.float32)
    hidden = residual.astype(jnp.float32) + attn_out
    scale_rows = lax.rsqrt(lax.optimization_barrier(jnp.mean(hidden * hidden, axis=1, keepdims=True)) + EPSILON)
    normed = (hidden * scale_rows * norm_gain).astype(jnp.bfloat16)
    grouped_ids = expert_ids.reshape(N_EXPERT, TOK_GRP * TOP)
    slots = jax.vmap(route_slots)(grouped_ids)
    group_index = jnp.arange(N_EXPERT, dtype=jnp.int32)[:, None]
    slot_index = (grouped_ids * (N_EXPERT * CAP) + group_index * CAP + slots).reshape(-1)
    source = jnp.arange(TOKENS * TOP, dtype=jnp.int32) // TOP
    buffer_rows = jnp.zeros((EXPERTS * N_EXPERT * CAP, D), jnp.bfloat16).at[slot_index].set(jnp.take(normed, source, axis=0))

    def expert_rows(inputs):
        rows_in, gate_mat, up_mat, down_mat = inputs
        gate_part = jnp.dot(rows_in, gate_mat, preferred_element_type=jnp.float32)
        up_part = jnp.dot(rows_in, up_mat, preferred_element_type=jnp.float32)
        active = (jax.nn.silu(gate_part) * up_part).astype(jnp.bfloat16)
        active = lax.optimization_barrier(active)
        pieces = jnp.einsum('rsf,sfd->rsd', active.reshape(-1, N_TENSOR, FF // N_TENSOR).astype(jnp.float32), down_mat.reshape(N_TENSOR, FF // N_TENSOR, D).astype(jnp.float32))
        slice_out = lax.optimization_barrier(pieces.astype(jnp.bfloat16))
        return lax.optimization_barrier(jnp.sum(slice_out.astype(jnp.float32), axis=1))
    expert_out = lax.map(expert_rows, (buffer_rows.reshape(EXPERTS, N_EXPERT * CAP, D), w_gate, w_up, w_down))
    routed = jnp.take(expert_out.reshape(EXPERTS * N_EXPERT * CAP, D), slot_index, axis=0)
    mixed_sum = lax.optimization_barrier(jnp.sum((routed * gate_weights.reshape(-1, 1)).reshape(TOKENS, TOP, D), axis=1))
    return (hidden + mixed_sum).astype(jnp.bfloat16)
```

```python
import jax
import jax.numpy as jnp
from jax import lax
from jax.experimental import pallas as pl
from jax.experimental.pallas import tpu as pltpu
from jax.sharding import PartitionSpec as P

GX, GY, GC = 4, 4, 2
LATENT = 512
ROPE = 64
VDIM = 128
EPSILON = 1e-06
LANES = 128


bf16 = jnp.bfloat16
f32 = jnp.float32


def place(x, y, c):
    return ((x % GX) * GY + y % GY) * GC + c % GC


def near(v, dx=0, dy=0, dc=0):
    pairs = [
        (place(x + dx, y + dy, c + dc), place(x, y, c))
        for x in range(GX)
        for y in range(GY)
        for c in range(GC)
    ]
    return lax.ppermute(v, "expert", pairs)


def far(v, dz):
    size = lax.axis_size("tensor")
    return lax.ppermute(v, "tensor", [((z + dz) % size, z) for z in range(size)])


def together(*values):
    return lax.optimization_barrier(values)


def rows_of(parts):
    return jnp.concatenate(parts, axis=0)


def plus(*terms):
    total = terms[0].astype(f32)
    for term in terms[1:]:
        total = total + term.astype(f32)
    return total


def padded(v, above, below):
    return jnp.pad(v, ((above, below), (0, 0)))


def gather_pair(a, b, axis_a, axis_b):
    a, b = together(a, b)
    a_after, a_before = near(a, **{axis_a: 1}), near(a, **{axis_a: -1})
    b_after, b_before = near(b, **{axis_b: 1}), near(b, **{axis_b: -1})
    half = a.shape[0] // 2
    parts = together(a_after[:half], a_before[half:], b_after[:half], b_before[half:])
    a_opposite = [near(parts[0], **{axis_a: 1}), near(parts[1], **{axis_a: -1})]
    b_opposite = [near(parts[2], **{axis_b: 1}), near(parts[3], **{axis_b: -1})]
    return (a, a_after, rows_of(a_opposite), a_before), (
        b,
        b_after,
        rows_of(b_opposite),
        b_before,
    )


def scatter_pair(a, b, axis_a, axis_b):
    half = a[0][0].shape[0] // 2
    opposite = []
    for terms in (a[2], b[2]):
        total = plus(*terms).astype(bf16)
        opposite += [total[:half], total[half:]]
    opposite = together(*opposite)
    via = [
        near(opposite[0], **{axis_a: -1}),
        near(opposite[1], **{axis_a: 1}),
        near(opposite[2], **{axis_b: -1}),
        near(opposite[3], **{axis_b: 1}),
    ]
    sent = []
    for i, terms in enumerate((a, b)):
        sent.append(plus(*terms[1], padded(via[2 * i], 0, half)).astype(bf16))
        sent.append(plus(*terms[3], padded(via[2 * i + 1], half, 0)).astype(bf16))
    sent = together(*sent)
    got = [
        near(sent[0], **{axis_a: -1}),
        near(sent[1], **{axis_a: 1}),
        near(sent[2], **{axis_b: -1}),
        near(sent[3], **{axis_b: 1}),
    ]
    return plus(*a[0], got[0], got[1]), plus(*b[0], got[2], got[3])


def expert_kernel(*refs, blocks, per_block):
    n = blocks * per_block
    pieces, (gates, w_gate, w_up, w_down), made = refs[:n], refs[n : n + 4], refs[n + 4 : 2 * n + 4]
    x, both, down, scale, active, y, x_sem, w_sem, o_sem = refs[2 * n + 4 :]
    rows = pieces[0].shape[0]
    local, width, ff = w_gate.shape
    step = 512
    x_copies = [
        pltpu.make_async_copy(
            pieces[i], x.at[i // per_block, pl.ds((i % per_block) * rows, rows)], x_sem.at[i]
        )
        for i in range(n)
    ]
    w_copies = []
    for e in range(local):
        w_copies.append(
            pltpu.make_async_copy(w_gate.at[e], both.at[e, :, pl.ds(0, ff)], w_sem.at[2 * e])
        )
        w_copies.append(
            pltpu.make_async_copy(w_up.at[e], both.at[e, :, pl.ds(ff, ff)], w_sem.at[2 * e + 1])
        )
    scale_copy = pltpu.make_async_copy(gates, scale, w_sem.at[2 * local])
    down_copy = pltpu.make_async_copy(w_down, down, w_sem.at[2 * local + 1])
    for copy in x_copies[:per_block] + w_copies[:2] + [scale_copy] + w_copies[2:]:
        copy.start()
    for copy in [down_copy] + x_copies[per_block:]:
        copy.start()
    out_copies = []
    for b in range(blocks):
        for copy in x_copies[b * per_block : (b + 1) * per_block]:
            copy.wait()
        if b == 0:
            scale_copy.wait()
        block_rows = per_block * rows
        for e in range(local):
            if b == 0:
                w_copies[2 * e].wait()
                w_copies[2 * e + 1].wait()
            parts = jnp.dot(x[b], both[e], preferred_element_type=f32)
            gate_part, up_part = parts[:, :ff], parts[:, ff:]
            value = gate_part / (1.0 + jnp.exp(-gate_part)) * up_part
            value = value * scale[pl.ds(b * block_rows, block_rows), pl.ds(e * ff, ff)]
            active[:, pl.ds(e * ff, ff)] = value.astype(bf16)
        if b == 0:
            down_copy.wait()
        for at in range(0, width, step):
            size = min(step, width - at)
            y[b, :, pl.ds(at, size)] = jnp.dot(
                active[...], down[:, pl.ds(at, size)], preferred_element_type=f32
            ).astype(bf16)
        for i in range(b * per_block, (b + 1) * per_block):
            copy = pltpu.make_async_copy(
                y.at[b, pl.ds((i % per_block) * rows, rows)], made[i], o_sem.at[i]
            )
            copy.start()
            out_copies.append(copy)
    for copy in out_copies:
        copy.wait()


def run_experts(pieces, gates, w_gate, w_up, w_down, per_block=4):
    n = len(pieces)
    blocks = n // per_block
    rows, width = pieces[0].shape
    local, _, ff = w_gate.shape
    hidden = local * ff
    anywhere = pl.BlockSpec(memory_space=pl.ANY)
    total = n * rows
    return pl.pallas_call(
        lambda *refs: expert_kernel(*refs, blocks=blocks, per_block=per_block),
        out_shape=[jax.ShapeDtypeStruct((rows, width), bf16)] * n,
        in_specs=[anywhere] * (n + 4),
        out_specs=[anywhere] * n,
        scratch_shapes=[
            pltpu.VMEM((blocks, per_block * rows, width), bf16),
            pltpu.VMEM((local, width, 2 * ff), bf16),
            pltpu.VMEM((hidden, width), bf16),
            pltpu.VMEM((total, hidden), f32),
            pltpu.VMEM((per_block * rows, hidden), bf16),
            pltpu.VMEM((blocks, per_block * rows, width), bf16),
            pltpu.SemaphoreType.DMA((n,)),
            pltpu.SemaphoreType.DMA((2 * local + 2,)),
            pltpu.SemaphoreType.DMA((n,)),
        ],
        cost_estimate=pl.CostEstimate(
            flops=6 * total * width * hidden,
            transcendentals=total * hidden,
            bytes_accessed=6 * width * hidden + 4 * total * width,
        ),
        name="experts",
    )(*pieces, gates, w_gate, w_up, w_down.reshape(hidden, width))


def z_scatter(parts):
    total = parts[0].astype(f32)
    for k in range(1, len(parts)):
        total = total + far(parts[k].astype(bf16), -k).astype(f32)
    return total


def attention(queries, latent_cache, new_latents):
    tok_rows = queries.shape[0]
    context = latent_cache.shape[0]
    key_rows = jnp.concatenate([latent_cache, new_latents], axis=0)
    scores = jnp.einsum("thc,kc->htk", queries, key_rows, preferred_element_type=f32) * (
        VDIM + ROPE
    ) ** (-0.5)
    query_pos = jnp.arange(tok_rows, dtype=jnp.int32)[:, None]
    key_pos = jnp.arange(key_rows.shape[0], dtype=jnp.int32)[None, :] - context
    scores = jnp.where((key_pos <= query_pos)[None], scores, -jnp.inf)
    row_peak = jnp.max(scores, axis=2, keepdims=True)
    exp_scores = jnp.exp(scores - row_peak)
    attn_probs = (exp_scores / jnp.sum(exp_scores, axis=2, keepdims=True)).astype(bf16)
    return jnp.einsum(
        "htk,kl->thl", attn_probs, key_rows[:, :LATENT], preferred_element_type=f32
    ).astype(bf16)


def onehot(target, size):
    return (jnp.arange(size, dtype=jnp.int32)[:, None] == target[None, :]).astype(bf16)


def per_device(
    queries,
    latent_cache,
    new_latents,
    residual,
    w_uv,
    w_out,
    norm_gain,
    expert_ids,
    gate_weights,
    w_gate,
    w_up,
    w_down,
):
    tok_rows, head_count = queries.shape[0], queries.shape[1]
    own_rows, width = residual.shape
    planes = lax.axis_size("tensor")
    local_experts, _, ff = w_gate.shape
    experts_all = local_experts * lax.axis_size("expert")
    at = lax.axis_index("expert")
    z = lax.axis_index("tensor")
    x, y, c = at // (GY * GC), (at // GC) % GY, at % GC

    turn = onehot((jnp.arange(tok_rows, dtype=jnp.int32) + own_rows * z) % tok_rows, tok_rows).T

    expert_row = jnp.arange(experts_all, dtype=jnp.int32)[None, :]
    dense = jnp.zeros((tok_rows, experts_all), f32)
    for k in range(expert_ids.shape[1]):
        dense = dense + jnp.where(
            expert_ids[:, k : k + 1] == expert_row, gate_weights[:, k : k + 1], 0.0
        )
    turned = jnp.dot(turn, dense.astype(bf16), preferred_element_type=f32).astype(bf16)

    per_owner = w_out.shape[0]
    tiles = width // LANES
    small = rows_of([w_uv, turned])
    extra = -(-small.shape[0] // (tiles * 8)) * 8
    uv_rows = w_uv.shape[0]
    small = padded(small, 0, tiles * extra - small.shape[0])
    small = small.reshape(tiles, extra, LANES).transpose(1, 0, 2).reshape(extra, width)
    block = per_owner + extra
    owners = GX * GY * GC
    weights = lax.all_gather(rows_of([w_out, small]), "expert", tiled=True)

    attended = attention(queries, latent_cache, new_latents)

    small_all = weights.reshape(owners, block, width)[:, per_owner:]
    small_all = small_all.reshape(owners, extra, tiles, LANES).transpose(0, 2, 1, 3)
    small_all = small_all.reshape(owners, tiles * extra, LANES)
    uv_heads = small_all[:, :uv_rows].reshape(head_count, LATENT, VDIM)
    head_values = jnp.einsum("thl,hlv->thv", attended, uv_heads, preferred_element_type=f32)
    head_values = head_values.astype(bf16).reshape(tok_rows, head_count * VDIM)
    head_values = jnp.dot(turn, head_values, preferred_element_type=f32).astype(bf16)

    place_of = jnp.arange(owners * block, dtype=jnp.int32)
    column = jnp.where(
        place_of % block < per_owner, place_of // block * per_owner + place_of % block, -1
    )
    spread = jnp.dot(
        head_values, onehot(column, head_count * VDIM), preferred_element_type=f32
    ).astype(bf16)
    partial = jnp.dot(spread, weights, preferred_element_type=f32)

    blocks = [partial[k * own_rows : (k + 1) * own_rows] for k in range(planes)]
    own_hidden = z_scatter(blocks) + residual.astype(f32)
    scale_rows = lax.rsqrt(jnp.mean(own_hidden * own_hidden, axis=1, keepdims=True) + EPSILON)
    own_normed = (own_hidden * scale_rows * norm_gain).astype(bf16)
    normed = [own_normed] + [far(own_normed, k) for k in range(1, planes)]

    gates = small_all[:, uv_rows : uv_rows + tok_rows].reshape(GX, GY, GC, tok_rows, LANES)
    gates = jnp.roll(jnp.roll(gates, -x, axis=0), -y, axis=1)
    gates = jnp.where(c == 0, gates, gates[:, :, ::-1])
    hidden_all = local_experts * ff
    chosen = onehot(
        at * local_experts + jnp.arange(hidden_all, dtype=jnp.int32) // ff, experts_all
    )
    half = tok_rows // 2

    def gate_rows(places):
        picked = []
        for i, j in places:
            for core in range(GC):
                for piece in (gates[:, i, core, :half], gates[j, :, core, half:]):
                    picked.append(piece.reshape(-1, LANES))
        return jnp.dot(rows_of(picked), chosen, preferred_element_type=f32)

    gates_1, gates_2, gates_3 = together(
        gate_rows([(0, 0)]), gate_rows([(1, 1), (3, 3)]), gate_rows([(2, 2)])
    )

    def experts(pairs, gate_scale):
        pieces = []
        for a, b in pairs:
            pieces += [a, b, near(a, dc=1), near(b, dc=1)]
        made = run_experts(pieces, gate_scale, w_gate, w_up, w_down)
        return [
            [made[4 * i + j], near(made[4 * i + 2 + j], dc=1)]
            for i in range(len(pairs))
            for j in range(2)
        ]

    rows_a, rows_b = rows_of(normed[: planes // 2]), rows_of(normed[planes // 2 :])
    all_a, all_b = gather_pair(rows_a, rows_b, "dx", "dy")
    block_a, block_b = together(rows_of(all_a), rows_of(all_b))
    all_a, all_b = gather_pair(block_a, block_b, "dy", "dx")
    own_a, own_b = experts([(all_a[0], all_b[0])], gates_1)
    after_a, after_b, before_a, before_b = experts(
        [(all_a[1], all_b[1]), (all_a[3], all_b[3])], gates_2
    )
    opposite_a, opposite_b = experts([(all_a[2], all_b[2])], gates_3)
    total_a, total_b = scatter_pair(
        (own_a, after_a, opposite_a, before_a), (own_b, after_b, opposite_b, before_b), "dy", "dx"
    )

    def fours(total):
        total = total.astype(bf16)
        return [[total[i * half : (i + 1) * half]] for i in range(4)]

    final = scatter_pair(fours(total_a), fours(total_b), "dx", "dy")
    blocks = [
        part[k * own_rows : (k + 1) * own_rows] for part in final for k in range(planes // 2)
    ]
    return (own_hidden + z_scatter(blocks)).astype(bf16)


def solution(mesh):
    placed = (
        P("expert", "tensor", None),
        P("expert", None),
        P("expert", None),
        P(("expert", "tensor"), None),
        P(("tensor", "expert"), None),
        P(("tensor", "expert"), None),
        P(),
        P("expert", None),
        P("expert", None),
        P("expert", None, "tensor"),
        P("expert", None, "tensor"),
        P("expert", "tensor", None),
    )

    return jax.shard_map(
        per_device,
        mesh=mesh,
        in_specs=placed,
        out_specs=P(("expert", "tensor"), None),
        check_vma=False,
    )
```

```python
import jax
import jax.numpy as jnp
from jax import lax
from jax.experimental import pallas as pl
from jax.experimental.pallas import tpu as pltpu
from jax.sharding import PartitionSpec as P

GX, GY, GC = 4, 4, 2
LATENT = 512
ROPE = 64
VDIM = 128
EPSILON = 1e-06
LANES = 128


bf16 = jnp.bfloat16
f32 = jnp.float32


def place(x, y, c):
    return ((x % GX) * GY + y % GY) * GC + c % GC


def near(v, dx=0, dy=0, dc=0):
    pairs = [
        (place(x + dx, y + dy, c + dc), place(x, y, c))
        for x in range(GX)
        for y in range(GY)
        for c in range(GC)
    ]
    return lax.ppermute(v, "expert", pairs)


def together(*values):
    return lax.optimization_barrier(values)


def rows_of(parts):
    return jnp.concatenate(parts, axis=0)


def plus(*terms):
    total = terms[0].astype(f32)
    for term in terms[1:]:
        total = total + term.astype(f32)
    return total


def padded(v, above, below):
    return jnp.pad(v, ((above, below), (0, 0)))


def gather_pair(a, b, axis_a, axis_b):
    a, b = together(a, b)
    a_after, a_before = near(a, **{axis_a: 1}), near(a, **{axis_a: -1})
    b_after, b_before = near(b, **{axis_b: 1}), near(b, **{axis_b: -1})
    half = a.shape[0] // 2
    parts = together(a_after[:half], a_before[half:], b_after[:half], b_before[half:])
    a_opposite = [near(parts[0], **{axis_a: 1}), near(parts[1], **{axis_a: -1})]
    b_opposite = [near(parts[2], **{axis_b: 1}), near(parts[3], **{axis_b: -1})]
    return (a, a_after, rows_of(a_opposite), a_before), (
        b,
        b_after,
        rows_of(b_opposite),
        b_before,
    )


def gather_direct(a, b, axis_a, axis_b):
    a, b = together(a, b)
    got_a = [a] + [near(a, **{axis_a: k}) for k in (1, 2, -1)]
    got_b = [b] + [near(b, **{axis_b: k}) for k in (1, 2, -1)]
    return together(rows_of(got_a), rows_of(got_b))


def scatter_direct(a, b, axis_a, axis_b):
    size = a.shape[0] // 4
    blocks = [v[i * size : (i + 1) * size] for v in (a, b) for i in range(4)]
    blocks = together(*blocks)
    sums = []
    for i, axis in ((0, axis_a), (4, axis_b)):
        got = [near(blocks[i + j], **{axis: -k}) for j, k in ((1, 1), (2, 2), (3, -1))]
        sums.append(plus(blocks[i], *got))
    return sums


def scatter_pair(a, b, axis_a, axis_b):
    half = a[0][0].shape[0] // 2
    opposite = []
    for terms in (a[2], b[2]):
        total = plus(*terms).astype(bf16)
        opposite += [total[:half], total[half:]]
    opposite = together(*opposite)
    via = [
        near(opposite[0], **{axis_a: -1}),
        near(opposite[1], **{axis_a: 1}),
        near(opposite[2], **{axis_b: -1}),
        near(opposite[3], **{axis_b: 1}),
    ]
    sent = []
    for i, terms in enumerate((a, b)):
        sent.append(plus(*terms[1], padded(via[2 * i], 0, half)).astype(bf16))
        sent.append(plus(*terms[3], padded(via[2 * i + 1], half, 0)).astype(bf16))
    sent = together(*sent)
    got = [
        near(sent[0], **{axis_a: -1}),
        near(sent[1], **{axis_a: 1}),
        near(sent[2], **{axis_b: -1}),
        near(sent[3], **{axis_b: 1}),
    ]
    return plus(*a[0], got[0], got[1]), plus(*b[0], got[2], got[3])


def pair_kernel(w_gate, w_up, both, sem):
    local, _, ff = w_gate.shape
    copies = []
    for e in range(local):
        for i, w in enumerate((w_gate, w_up)):
            copies.append(
                pltpu.make_async_copy(w.at[e], both.at[e, :, pl.ds(i * ff, ff)], sem.at[2 * e + i])
            )
    for copy in copies:
        copy.start()
    for copy in copies:
        copy.wait()


def side_by_side(w_gate, w_up):
    local, width, ff = w_gate.shape
    anywhere = pl.BlockSpec(memory_space=pl.ANY)
    return pl.pallas_call(
        pair_kernel,
        out_shape=jax.ShapeDtypeStruct((local, width, 2 * ff), w_gate.dtype),
        in_specs=[anywhere] * 2,
        out_specs=anywhere,
        scratch_shapes=[pltpu.SemaphoreType.DMA((2 * local,))],
        cost_estimate=pl.CostEstimate(
            flops=0, transcendentals=0, bytes_accessed=8 * local * width * ff
        ),
        name="side_by_side",
    )(w_gate, w_up)


def expert_kernel(*refs, blocks):
    n = 4 * blocks
    pieces, (gates, both, down, own, other) = refs[:n], refs[n : n + 5]
    x, scale, active, y, x_sem, s_sem, o_sem = refs[n + 5 :]
    rows, width = pieces[0].shape
    local, _, ff = both.shape
    ff = ff // 2
    step = 512
    scale_copy = pltpu.make_async_copy(gates, scale, s_sem)
    x_copies = [
        pltpu.make_async_copy(pieces[i], x.at[i // 4, pl.ds(i % 4 * rows, rows)], x_sem.at[i])
        for i in range(n)
    ]
    for copy in x_copies[:4] + [scale_copy] + x_copies[4:]:
        copy.start()
    out_copies = []
    for b in range(blocks):
        for copy in x_copies[4 * b : 4 * b + 4]:
            copy.wait()
        if b == 0:
            scale_copy.wait()
        for e in range(local):
            parts = jnp.dot(x[b], both[e], preferred_element_type=f32)
            gate_part, up_part = parts[:, :ff], parts[:, ff:]
            value = gate_part / (1.0 + jnp.exp(-gate_part)) * up_part
            value = value * scale[pl.ds(4 * b * rows, 4 * rows), pl.ds(e * ff, ff)]
            active[:, pl.ds(e * ff, ff)] = value.astype(bf16)
        for at in range(0, width, step):
            size = min(step, width - at)
            y[b, :, pl.ds(at, size)] = jnp.dot(
                active[...], down[:, pl.ds(at, size)], preferred_element_type=f32
            ).astype(bf16)
        for i in range(4):
            copy = pltpu.make_async_copy(
                y.at[b, pl.ds(i * rows, rows)],
                (own, other)[i // 2].at[2 * b + i % 2],
                o_sem.at[4 * b + i],
            )
            copy.start()
            out_copies.append(copy)
    for copy in out_copies:
        copy.wait()


def run_experts(pieces, gates, both, down):
    blocks = len(pieces) // 4
    rows, width = pieces[0].shape
    hidden = down.shape[0]
    total = 4 * blocks * rows
    anywhere = pl.BlockSpec(memory_space=pl.ANY)
    on_chip = pl.BlockSpec(memory_space=pltpu.VMEM)
    return pl.pallas_call(
        lambda *refs: expert_kernel(*refs, blocks=blocks),
        out_shape=[jax.ShapeDtypeStruct((2 * blocks, rows, width), bf16)] * 2,
        in_specs=[anywhere] * (len(pieces) + 1) + [on_chip] * 2,
        out_specs=[anywhere] * 2,
        scratch_shapes=[
            pltpu.VMEM((blocks, 4 * rows, width), bf16),
            pltpu.VMEM((total, hidden), f32),
            pltpu.VMEM((4 * rows, hidden), bf16),
            pltpu.VMEM((blocks, 4 * rows, width), bf16),
            pltpu.SemaphoreType.DMA((4 * blocks,)),
            pltpu.SemaphoreType.DMA,
            pltpu.SemaphoreType.DMA((4 * blocks,)),
        ],
        compiler_params=pltpu.CompilerParams(vmem_limit_bytes=(20 if blocks == 1 else 32) << 20),
        cost_estimate=pl.CostEstimate(
            flops=6 * total * width * hidden,
            transcendentals=total * hidden,
            bytes_accessed=4 * total * width,
        ),
        name="experts",
    )(*pieces, gates, both, down)


def z_scatter(rows):
    parts = rows.astype(bf16).reshape(lax.axis_size("tensor"), -1, rows.shape[1])
    arrived = lax.all_to_all(parts, "tensor", split_axis=0, concat_axis=0, tiled=True)
    return arrived.astype(f32).sum(axis=0)


def z_gather(rows):
    parts = jnp.broadcast_to(rows[None], (lax.axis_size("tensor"), *rows.shape))
    arrived = lax.all_to_all(parts, "tensor", split_axis=0, concat_axis=0, tiled=True)
    return arrived.reshape(-1, rows.shape[1])


def attention(queries, latent_cache, new_latents):
    tok_rows = queries.shape[0]
    context = latent_cache.shape[0]
    key_rows = jnp.concatenate([latent_cache, new_latents], axis=0)
    scores = jnp.einsum("thc,kc->htk", queries, key_rows, preferred_element_type=f32) * (
        VDIM + ROPE
    ) ** (-0.5)
    query_pos = jnp.arange(tok_rows, dtype=jnp.int32)[:, None]
    key_pos = jnp.arange(key_rows.shape[0], dtype=jnp.int32)[None, :] - context
    scores = jnp.where((key_pos <= query_pos)[None], scores, -jnp.inf)
    row_peak = jnp.max(scores, axis=2, keepdims=True)
    exp_scores = jnp.exp(scores - row_peak)
    attn_probs = (exp_scores / jnp.sum(exp_scores, axis=2, keepdims=True)).astype(bf16)
    return jnp.einsum(
        "htk,kl->thl", attn_probs, key_rows[:, :LATENT], preferred_element_type=f32
    ).astype(bf16)


def onehot(target, size):
    return (jnp.arange(size, dtype=jnp.int32)[:, None] == target[None, :]).astype(bf16)


def per_device(
    queries,
    latent_cache,
    new_latents,
    residual,
    w_uv,
    w_out,
    norm_gain,
    expert_ids,
    gate_weights,
    w_gate,
    w_up,
    w_down,
):
    tok_rows, head_count = queries.shape[0], queries.shape[1]
    _, width = residual.shape
    local_experts, _, ff = w_gate.shape
    experts_all = local_experts * lax.axis_size("expert")
    at = lax.axis_index("expert")
    x, y, c = at // (GY * GC), (at // GC) % GY, at % GC

    expert_row = jnp.arange(experts_all, dtype=jnp.int32)[None, :]
    dense = jnp.zeros((tok_rows, experts_all), f32)
    for k in range(expert_ids.shape[1]):
        dense = dense + jnp.where(
            expert_ids[:, k : k + 1] == expert_row, gate_weights[:, k : k + 1], 0.0
        )

    per_owner = w_out.shape[0]
    tiles = width // LANES
    small = rows_of([w_uv, dense.astype(bf16)])
    extra = -(-small.shape[0] // (tiles * 8)) * 8
    uv_rows = w_uv.shape[0]
    small = padded(small, 0, tiles * extra - small.shape[0])
    small = small.reshape(tiles, extra, LANES).transpose(1, 0, 2).reshape(extra, width)
    block = per_owner + extra
    owners = GX * GY * GC
    weights = lax.all_gather(rows_of([w_out, small]), "expert", tiled=True)
    both = side_by_side(w_gate, w_up)

    attended = attention(queries, latent_cache, new_latents)

    small_all = weights.reshape(owners, block, width)[:, per_owner:]
    small_all = small_all.reshape(owners, extra, tiles, LANES).transpose(0, 2, 1, 3)
    small_all = small_all.reshape(owners, tiles * extra, LANES)
    uv_heads = small_all[:, :uv_rows].reshape(head_count, LATENT, VDIM)
    head_values = jnp.einsum("thl,hlv->thv", attended, uv_heads, preferred_element_type=f32)
    head_values = head_values.astype(bf16).reshape(tok_rows, head_count * VDIM)

    place_of = jnp.arange(owners * block, dtype=jnp.int32)
    column = jnp.where(
        place_of % block < per_owner, place_of // block * per_owner + place_of % block, -1
    )
    spread = jnp.dot(
        head_values, onehot(column, head_count * VDIM), preferred_element_type=f32
    ).astype(bf16)
    partial = jnp.dot(spread, weights, preferred_element_type=f32)

    own_hidden = z_scatter(partial) + residual.astype(f32)
    scale_rows = lax.rsqrt(jnp.mean(own_hidden * own_hidden, axis=1, keepdims=True) + EPSILON)
    own_normed = (own_hidden * scale_rows * norm_gain).astype(bf16)
    normed = z_gather(own_normed)

    gates = small_all[:, uv_rows : uv_rows + tok_rows].reshape(GX, GY, GC, tok_rows, LANES)
    gates = jnp.roll(jnp.roll(gates, -x, axis=0), -y, axis=1)
    gates = jnp.where(c == 0, gates, gates[:, :, ::-1])
    hidden_all = local_experts * ff
    chosen = onehot(
        at * local_experts + jnp.arange(hidden_all, dtype=jnp.int32) // ff, experts_all
    )
    half = tok_rows // 2

    def gate_rows(places):
        picked = []
        for i, j in places:
            for core in range(GC):
                for piece in (gates[:, i, core, :half], gates[j, :, core, half:]):
                    picked.append(piece.reshape(-1, LANES))
        return jnp.dot(rows_of(picked), chosen, preferred_element_type=f32)

    down_mat = w_down.reshape(hidden_all, width)
    gates_1, gates_2, gates_3 = together(
        gate_rows([(0, 0)]), gate_rows([(1, 1), (3, 3)]), gate_rows([(2, 2)])
    )

    def experts(pairs, gate_scale):
        pieces = []
        for a, b in pairs:
            pieces += [a, b, near(a, dc=1), near(b, dc=1)]
        own, other = run_experts(pieces, gate_scale, both, down_mat)
        other = near(other, dc=1)
        return [[own[i], other[i]] for i in range(2 * len(pairs))]

    block_a, block_b = gather_direct(normed[:half], normed[half:], "dx", "dy")
    all_a, all_b = gather_pair(block_a, block_b, "dy", "dx")
    own_a, own_b = experts([(all_a[0], all_b[0])], gates_1)
    after_a, after_b, before_a, before_b = experts(
        [(all_a[1], all_b[1]), (all_a[3], all_b[3])], gates_2
    )
    opposite_a, opposite_b = experts([(all_a[2], all_b[2])], gates_3)
    total_a, total_b = scatter_pair(
        (own_a, after_a, opposite_a, before_a), (own_b, after_b, opposite_b, before_b), "dy", "dx"
    )

    final = scatter_direct(total_a.astype(bf16), total_b.astype(bf16), "dx", "dy")
    return (own_hidden + z_scatter(rows_of(final))).astype(bf16)


def solution(mesh):
    placed = (
        P("expert", "tensor", None),
        P("expert", None),
        P("expert", None),
        P(("expert", "tensor"), None),
        P(("tensor", "expert"), None),
        P(("tensor", "expert"), None),
        P(),
        P("expert", None),
        P("expert", None),
        P("expert", None, "tensor"),
        P("expert", None, "tensor"),
        P("expert", "tensor", None),
    )

    return jax.shard_map(
        per_device,
        mesh=mesh,
        in_specs=placed,
        out_specs=P(("expert", "tensor"), None),
        check_vma=False,
    )
```

```python
import jax
import jax.numpy as jnp
from jax import lax
from jax.experimental import pallas as pl
from jax.experimental.pallas import tpu as pltpu
from jax.sharding import PartitionSpec as P

GX, GY, GC = 4, 4, 2
LATENT = 512
ROPE = 64
VDIM = 128
EPSILON = 1e-06
LANES = 128


bf16 = jnp.bfloat16
f32 = jnp.float32


def place(x, y, c):
    return ((x % GX) * GY + y % GY) * GC + c % GC


def near(v, dx=0, dy=0, dc=0):
    pairs = [
        (place(x + dx, y + dy, c + dc), place(x, y, c))
        for x in range(GX)
        for y in range(GY)
        for c in range(GC)
    ]
    return lax.ppermute(v, "expert", pairs)


def together(*values):
    return lax.optimization_barrier(values)


def rows_of(parts):
    return jnp.concatenate(parts, axis=0)


def plus(*terms):
    total = terms[0].astype(f32)
    for term in terms[1:]:
        total = total + term.astype(f32)
    return total


def padded(v, above, below):
    return jnp.pad(v, ((above, below), (0, 0)))


def gather_pair(a, b, axis_a, axis_b):
    a, b = together(a, b)
    a_after, a_before = near(a, **{axis_a: 1}), near(a, **{axis_a: -1})
    b_after, b_before = near(b, **{axis_b: 1}), near(b, **{axis_b: -1})
    half = a.shape[0] // 2
    parts = together(a_after[:half], a_before[half:], b_after[:half], b_before[half:])
    a_opposite = [near(parts[0], **{axis_a: 1}), near(parts[1], **{axis_a: -1})]
    b_opposite = [near(parts[2], **{axis_b: 1}), near(parts[3], **{axis_b: -1})]
    return (a, a_after, a_opposite, a_before), (b, b_after, b_opposite, b_before)


def gather_direct(a, b, axis_a, axis_b):
    a, b = together(a, b)
    got = [near(a, **{axis_a: k}) for k in (1, 2, -1)]
    got += [near(b, **{axis_b: k}) for k in (1, 2, -1)]
    got = together(*got)
    return together(rows_of([a, *got[:3]]), rows_of([b, *got[3:]]))


def scatter_direct(a, b, axis_a, axis_b):
    size = a.shape[0] // 4
    blocks = [v[i * size : (i + 1) * size] for v in (a, b) for i in range(4)]
    blocks = together(*blocks)
    sums = []
    for i, axis in ((0, axis_a), (4, axis_b)):
        got = [near(blocks[i + j], **{axis: -k}) for j, k in ((1, 1), (2, 2), (3, -1))]
        sums.append(plus(blocks[i], *got))
    return sums


def scatter_pair(a, b, axis_a, axis_b):
    half = a[0][0].shape[0] // 2
    opposite = []
    for terms in (a[2], b[2]):
        total = plus(*terms).astype(bf16)
        opposite += [total[:half], total[half:]]
    opposite = together(*opposite)
    via = [
        near(opposite[0], **{axis_a: -1}),
        near(opposite[1], **{axis_a: 1}),
        near(opposite[2], **{axis_b: -1}),
        near(opposite[3], **{axis_b: 1}),
    ]
    sent = []
    for i, terms in enumerate((a, b)):
        sent.append(plus(*terms[1], padded(via[2 * i], 0, half)).astype(bf16))
        sent.append(plus(*terms[3], padded(via[2 * i + 1], half, 0)).astype(bf16))
    sent = together(*sent)
    got = [
        near(sent[0], **{axis_a: -1}),
        near(sent[1], **{axis_a: 1}),
        near(sent[2], **{axis_b: -1}),
        near(sent[3], **{axis_b: 1}),
    ]
    return plus(*a[0], got[0], got[1]), plus(*b[0], got[2], got[3])


def expert_kernel(*refs, blocks, count):
    pieces, (gates, both, down, own, other) = refs[:count], refs[count : count + 5]
    x, scale, active, y, x_sem, s_sem, o_sem = refs[count + 5 :]
    per_block = count // blocks
    rows, width = pieces[0].shape
    out_rows = own.shape[1]
    block_rows = per_block * rows
    local, _, ff = both.shape
    ff = ff // 2
    step = 512
    scale_copy = pltpu.make_async_copy(gates, scale, s_sem)
    x_copies = [
        pltpu.make_async_copy(
            pieces[i], x.at[i // per_block, pl.ds(i % per_block * rows, rows)], x_sem.at[i]
        )
        for i in range(count)
    ]
    for copy in x_copies[:per_block] + [scale_copy] + x_copies[per_block:]:
        copy.start()
    out_copies = []
    for b in range(blocks):
        for copy in x_copies[per_block * b : per_block * (b + 1)]:
            copy.wait()
        if b == 0:
            scale_copy.wait()
        for e in range(local):
            parts = jnp.dot(x[b], both[e], preferred_element_type=f32)
            gate_part, up_part = parts[:, :ff], parts[:, ff:]
            value = gate_part / (1.0 + jnp.exp(-gate_part)) * up_part
            value = value * scale[pl.ds(b * block_rows, block_rows), pl.ds(e * ff, ff)]
            active[:, pl.ds(e * ff, ff)] = value.astype(bf16)
        for at in range(0, width, step):
            size = min(step, width - at)
            y[b, :, pl.ds(at, size)] = jnp.dot(
                active[...], down[:, pl.ds(at, size)], preferred_element_type=f32
            ).astype(bf16)
        for i in range(4):
            copy = pltpu.make_async_copy(
                y.at[b, pl.ds(i * out_rows, out_rows)],
                (own, other)[i // 2].at[2 * b + i % 2],
                o_sem.at[4 * b + i],
            )
            copy.start()
            out_copies.append(copy)
    for copy in out_copies:
        copy.wait()


def run_experts(pieces, gates, both, down, blocks):
    count = len(pieces)
    rows, width = pieces[0].shape
    hidden = down.shape[0]
    total = count * rows
    block_rows = total // blocks
    in_hbm = pl.BlockSpec(memory_space=pltpu.HBM)
    on_chip = pl.BlockSpec(memory_space=pltpu.VMEM)
    return pl.pallas_call(
        lambda *refs: expert_kernel(*refs, blocks=blocks, count=count),
        out_shape=[jax.ShapeDtypeStruct((2 * blocks, block_rows // 4, width), bf16)] * 2,
        in_specs=[in_hbm] * (count + 1) + [on_chip] * 2,
        out_specs=[in_hbm] * 2,
        scratch_shapes=[
            pltpu.VMEM((blocks, block_rows, width), bf16),
            pltpu.VMEM((total, hidden), f32),
            pltpu.VMEM((block_rows, hidden), bf16),
            pltpu.VMEM((blocks, block_rows, width), bf16),
            pltpu.SemaphoreType.DMA((count,)),
            pltpu.SemaphoreType.DMA,
            pltpu.SemaphoreType.DMA((4 * blocks,)),
        ],
        compiler_params=pltpu.CompilerParams(vmem_limit_bytes=(20 if blocks == 1 else 32) << 20),
        cost_estimate=pl.CostEstimate(
            flops=6 * total * width * hidden,
            transcendentals=total * hidden,
            bytes_accessed=4 * total * width,
        ),
        name="experts",
    )(*pieces, gates, both, down)


def z_scatter(rows):
    parts = rows.astype(bf16).reshape(lax.axis_size("tensor"), -1, rows.shape[1])
    arrived = lax.all_to_all(parts, "tensor", split_axis=0, concat_axis=0, tiled=True)
    return arrived.astype(f32).sum(axis=0)


def z_gather(rows):
    parts = jnp.broadcast_to(rows[None], (lax.axis_size("tensor"), *rows.shape))
    arrived = lax.all_to_all(parts, "tensor", split_axis=0, concat_axis=0, tiled=True)
    return arrived.reshape(-1, rows.shape[1])


def attention(queries, latent_cache, new_latents):
    tok_rows = queries.shape[0]
    context = latent_cache.shape[0]
    key_rows = jnp.concatenate([latent_cache, new_latents], axis=0)
    scores = jnp.einsum("thc,kc->htk", queries, key_rows, preferred_element_type=f32) * (
        VDIM + ROPE
    ) ** (-0.5)
    query_pos = jnp.arange(tok_rows, dtype=jnp.int32)[:, None]
    key_pos = jnp.arange(key_rows.shape[0], dtype=jnp.int32)[None, :] - context
    scores = jnp.where((key_pos <= query_pos)[None], scores, -jnp.inf)
    row_peak = jnp.max(scores, axis=2, keepdims=True)
    exp_scores = jnp.exp(scores - row_peak)
    attn_probs = (exp_scores / jnp.sum(exp_scores, axis=2, keepdims=True)).astype(bf16)
    return jnp.einsum(
        "htk,kl->thl", attn_probs, key_rows[:, :LATENT], preferred_element_type=f32
    ).astype(bf16)


def onehot(target, size):
    return (jnp.arange(size, dtype=jnp.int32)[:, None] == target[None, :]).astype(bf16)


def per_device(
    queries,
    latent_cache,
    new_latents,
    residual,
    w_uv,
    w_out,
    norm_gain,
    expert_ids,
    gate_weights,
    w_gate,
    w_up,
    w_down,
):
    tok_rows, head_count = queries.shape[0], queries.shape[1]
    _, width = residual.shape
    local_experts, _, ff = w_gate.shape
    experts_all = local_experts * lax.axis_size("expert")
    at = lax.axis_index("expert")
    x, y, c = at // (GY * GC), (at // GC) % GY, at % GC

    expert_row = jnp.arange(experts_all, dtype=jnp.int32)[None, :]
    dense = jnp.zeros((tok_rows, experts_all), f32)
    for k in range(expert_ids.shape[1]):
        dense = dense + jnp.where(
            expert_ids[:, k : k + 1] == expert_row, gate_weights[:, k : k + 1], 0.0
        )

    per_owner = w_out.shape[0]
    tiles = width // LANES
    small = rows_of([w_uv, dense.astype(bf16)])
    extra = -(-small.shape[0] // (tiles * 8)) * 8
    uv_rows = w_uv.shape[0]
    small = padded(small, 0, tiles * extra - small.shape[0])
    small = small.reshape(tiles, extra, LANES).transpose(1, 0, 2).reshape(extra, width)
    block = per_owner + extra
    owners = GX * GY * GC
    weights = lax.all_gather(rows_of([w_out, small]), "expert", tiled=True)
    both = together(jnp.concatenate([w_gate, w_up], axis=2))[0]

    attended = attention(queries, latent_cache, new_latents)

    small_all = weights.reshape(owners, block, width)[:, per_owner:]
    small_all = small_all.reshape(owners, extra, tiles, LANES).transpose(0, 2, 1, 3)
    small_all = small_all.reshape(owners, tiles * extra, LANES)
    uv_heads = small_all[:, :uv_rows].reshape(head_count, LATENT, VDIM)
    head_values = jnp.einsum("thl,hlv->thv", attended, uv_heads, preferred_element_type=f32)
    head_values = head_values.astype(bf16).reshape(tok_rows, head_count * VDIM)

    place_of = jnp.arange(owners * block, dtype=jnp.int32)
    column = jnp.where(
        place_of % block < per_owner, place_of // block * per_owner + place_of % block, -1
    )
    spread = jnp.dot(
        head_values, onehot(column, head_count * VDIM), preferred_element_type=f32
    ).astype(bf16)
    partial = jnp.dot(spread, weights, preferred_element_type=f32)

    gates = small_all[:, uv_rows : uv_rows + tok_rows].reshape(GX, GY, GC, tok_rows, LANES)
    gates = jnp.roll(jnp.roll(gates, -x, axis=0), -y, axis=1)
    gates = jnp.where(c == 0, gates, gates[:, :, ::-1])
    hidden_all = local_experts * ff
    chosen = onehot(
        at * local_experts + jnp.arange(hidden_all, dtype=jnp.int32) // ff, experts_all
    )
    half = tok_rows // 2

    def gate_rows(places):
        picked = []
        for i, j in places:
            for core in range(GC):
                for piece in (gates[:, i, core, :half], gates[j, :, core, half:]):
                    picked.append(piece.reshape(-1, LANES))
        return jnp.dot(rows_of(picked), chosen, preferred_element_type=f32)

    down_mat = w_down.reshape(hidden_all, width)
    partial, gates_1, gates_2, gates_3 = together(
        partial.astype(bf16),
        gate_rows([(0, 0)]),
        gate_rows([(1, 1), (3, 3)]),
        gate_rows([(2, 2)]),
    )

    own_hidden = z_scatter(partial) + residual.astype(f32)
    scale_rows = lax.rsqrt(jnp.mean(own_hidden * own_hidden, axis=1, keepdims=True) + EPSILON)
    own_normed = (own_hidden * scale_rows * norm_gain).astype(bf16)
    normed = z_gather(own_normed)

    def experts(blocks, gate_scale):
        pieces = []
        for block in blocks:
            pieces += block + [near(piece, dc=1) for piece in block]
        own, other = run_experts(pieces, gate_scale, both, down_mat, len(blocks))
        other = near(other, dc=1)
        return [[own[i], other[i]] for i in range(2 * len(blocks))]

    block_a, block_b = gather_direct(normed[:half], normed[half:], "dx", "dy")
    all_a, all_b = gather_pair(block_a, block_b, "dy", "dx")
    own_a, own_b = experts([[all_a[0], all_b[0]]], gates_1)
    after_a, after_b, before_a, before_b = experts(
        [[all_a[1], all_b[1]], [all_a[3], all_b[3]]], gates_2
    )
    opposite_a, opposite_b = experts([all_a[2] + all_b[2]], gates_3)
    total_a, total_b = scatter_pair(
        (own_a, after_a, opposite_a, before_a), (own_b, after_b, opposite_b, before_b), "dy", "dx"
    )

    final = scatter_direct(total_a.astype(bf16), total_b.astype(bf16), "dx", "dy")
    return (own_hidden + z_scatter(rows_of(final))).astype(bf16)


def solution(mesh):
    placed = (
        P("expert", "tensor", None),
        P("expert", None),
        P("expert", None),
        P(("expert", "tensor"), None),
        P(("tensor", "expert"), None),
        P(("tensor", "expert"), None),
        P(),
        P("expert", None),
        P("expert", None),
        P("expert", None, "tensor"),
        P("expert", None, "tensor"),
        P("expert", "tensor", None),
    )

    return jax.shard_map(
        per_device,
        mesh=mesh,
        in_specs=placed,
        out_specs=P(("expert", "tensor"), None),
        check_vma=False,
    )
```

```python
import jax
import jax.numpy as jnp
from jax import lax
from jax.experimental import pallas as pl
from jax.experimental.pallas import tpu as pltpu
from jax.sharding import PartitionSpec as P

GX, GY, GC = 4, 4, 2
LATENT = 512
ROPE = 64
VDIM = 128
EPSILON = 1e-06
LANES = 128


bf16 = jnp.bfloat16
f32 = jnp.float32


def place(x, y, c):
    return ((x % GX) * GY + y % GY) * GC + c % GC


def near(v, dx=0, dy=0, dc=0):
    pairs = [
        (place(x + dx, y + dy, c + dc), place(x, y, c))
        for x in range(GX)
        for y in range(GY)
        for c in range(GC)
    ]
    return lax.ppermute(v, "expert", pairs)


def together(*values):
    return lax.optimization_barrier(values)


def rows_of(parts):
    return jnp.concatenate(parts, axis=0)


def plus(*terms):
    total = terms[0].astype(f32)
    for term in terms[1:]:
        total = total + term.astype(f32)
    return total


def padded(v, above, below):
    return jnp.pad(v, ((above, below), (0, 0)))


def gather_pair(a, b, axis_a, axis_b):
    a_after, a_before = near(a[0], **{axis_a: 1}), near(a[1], **{axis_a: -1})
    b_after, b_before = near(b[0], **{axis_b: 1}), near(b[1], **{axis_b: -1})
    a_rest = near(a[1], **{axis_a: 1}), near(a[0], **{axis_a: -1})
    b_rest = near(b[1], **{axis_b: 1}), near(b[0], **{axis_b: -1})
    a_opposite = [near(a_after, **{axis_a: 1}), near(a_before, **{axis_a: -1})]
    b_opposite = [near(b_after, **{axis_b: 1}), near(b_before, **{axis_b: -1})]
    return (a, [a_after, a_rest[0]], a_opposite, [a_rest[1], a_before]), (
        b,
        [b_after, b_rest[0]],
        b_opposite,
        [b_rest[1], b_before],
    )


def gather_direct(a, b, axis_a, axis_b):
    a, b = together(a, b)
    got = [near(a, **{axis_a: k}) for k in (1, 2, -1)]
    got += [near(b, **{axis_b: k}) for k in (1, 2, -1)]
    got = together(*got)
    halves = [a, got[0]], [got[1], got[2]], [b, got[3]], [got[4], got[5]]
    halves = together(*(rows_of(half) for half in halves))
    return halves[:2], halves[2:]


def scatter_direct(a, b, axis_a, axis_b):
    size = a[0].shape[0] // 2
    blocks = [v[i * size : (i + 1) * size].astype(bf16) for v in (*a, *b) for i in range(2)]
    blocks = together(*blocks)
    sums = []
    for i, axis in ((0, axis_a), (4, axis_b)):
        got = [near(blocks[i + j], **{axis: -k}) for j, k in ((1, 1), (2, 2), (3, -1))]
        sums.append(plus(blocks[i], *got))
    return sums


def scatter_pair(a, b, axis_a, axis_b):
    half = a[0][0].shape[0] // 2

    def part(terms, second):
        cut = slice(half, None) if second else slice(0, half)
        return plus(*(term[cut] for term in terms))

    both = ((a, axis_a), (b, axis_b))
    opposite = together(*(part(v[2], i).astype(bf16) for v, _ in both for i in range(2)))
    via = [
        near(opposite[2 * n + i], **{axis: 2 * i - 1})
        for n, (_, axis) in enumerate(both)
        for i in range(2)
    ]
    plain = together(
        *(part(v[k], second).astype(bf16) for v, _ in both for k, second in ((1, 1), (3, 0)))
    )
    got = [
        near(plain[2 * n + i], **{axis: 2 * i - 1})
        for n, (_, axis) in enumerate(both)
        for i in range(2)
    ]
    merged = [
        (part(v[k], second) + via[2 * n + second].astype(f32)).astype(bf16)
        for n, (v, _) in enumerate(both)
        for k, second in ((1, 0), (3, 1))
    ]
    merged = together(*merged)
    last = [
        near(merged[2 * n + i], **{axis: 2 * i - 1})
        for n, (_, axis) in enumerate(both)
        for i in range(2)
    ]
    return [
        (
            part(v[0], 0) + plus(last[2 * n], got[2 * n + 1]),
            part(v[0], 1) + plus(got[2 * n], last[2 * n + 1]),
        )
        for n, (v, _) in enumerate(both)
    ]


def expert_kernel(*refs, blocks, count):
    pieces, (gates, both, down, own, other) = refs[:count], refs[count : count + 5]
    x, scale, active, y, x_sem, s_sem, o_sem = refs[count + 5 :]
    per_block = count // blocks
    rows, width = pieces[0].shape
    out_rows = own.shape[1]
    block_rows = per_block * rows
    local, _, ff = both.shape
    ff = ff // 2
    step = 512
    scale_copy = pltpu.make_async_copy(gates, scale, s_sem)
    x_copies = [
        pltpu.make_async_copy(
            pieces[i], x.at[i // per_block, pl.ds(i % per_block * rows, rows)], x_sem.at[i]
        )
        for i in range(count)
    ]
    for copy in x_copies[:per_block] + [scale_copy] + x_copies[per_block:]:
        copy.start()
    out_copies = []
    for b in range(blocks):
        for copy in x_copies[per_block * b : per_block * (b + 1)]:
            copy.wait()
        if b == 0:
            scale_copy.wait()
        for e in range(local):
            parts = jnp.dot(x[b], both[e], preferred_element_type=f32)
            gate_part, up_part = parts[:, :ff], parts[:, ff:]
            value = gate_part / (1.0 + jnp.exp(-gate_part)) * up_part
            value = value * scale[pl.ds(b * block_rows, block_rows), pl.ds(e * ff, ff)]
            active[:, pl.ds(e * ff, ff)] = value.astype(bf16)
        for at in range(0, width, step):
            size = min(step, width - at)
            y[b, :, pl.ds(at, size)] = jnp.dot(
                active[...], down[:, pl.ds(at, size)], preferred_element_type=f32
            ).astype(bf16)
        for i in range(4):
            copy = pltpu.make_async_copy(
                y.at[b, pl.ds(i * out_rows, out_rows)],
                (own, other)[i // 2].at[2 * b + i % 2],
                o_sem.at[4 * b + i],
            )
            copy.start()
            out_copies.append(copy)
    for copy in out_copies:
        copy.wait()


def run_experts(pieces, gates, both, down, blocks):
    count = len(pieces)
    rows, width = pieces[0].shape
    hidden = down.shape[0]
    total = count * rows
    block_rows = total // blocks
    in_hbm = pl.BlockSpec(memory_space=pltpu.HBM)
    on_chip = pl.BlockSpec(memory_space=pltpu.VMEM)
    return pl.pallas_call(
        lambda *refs: expert_kernel(*refs, blocks=blocks, count=count),
        out_shape=[jax.ShapeDtypeStruct((2 * blocks, block_rows // 4, width), bf16)] * 2,
        in_specs=[in_hbm] * (count + 1) + [on_chip] * 2,
        out_specs=[in_hbm] * 2,
        scratch_shapes=[
            pltpu.VMEM((blocks, block_rows, width), bf16),
            pltpu.VMEM((total, hidden), f32),
            pltpu.VMEM((block_rows, hidden), bf16),
            pltpu.VMEM((blocks, block_rows, width), bf16),
            pltpu.SemaphoreType.DMA((count,)),
            pltpu.SemaphoreType.DMA,
            pltpu.SemaphoreType.DMA((4 * blocks,)),
        ],
        compiler_params=pltpu.CompilerParams(vmem_limit_bytes=(14 if blocks == 1 else 24) << 20),
        cost_estimate=pl.CostEstimate(
            flops=6 * total * width * hidden,
            transcendentals=total * hidden,
            bytes_accessed=4 * total * width,
        ),
        name="experts",
    )(*pieces, gates, both, down)


def z_scatter(rows):
    parts = rows.astype(bf16).reshape(lax.axis_size("tensor"), -1, rows.shape[1])
    arrived = lax.all_to_all(parts, "tensor", split_axis=0, concat_axis=0, tiled=True)
    return arrived.astype(f32).sum(axis=0)


def z_gather(rows):
    parts = jnp.broadcast_to(rows[None], (lax.axis_size("tensor"), *rows.shape))
    arrived = lax.all_to_all(parts, "tensor", split_axis=0, concat_axis=0, tiled=True)
    return arrived.reshape(-1, rows.shape[1])


def attention(queries, latent_cache, new_latents):
    tok_rows = queries.shape[0]
    context = latent_cache.shape[0]
    key_rows = jnp.concatenate([latent_cache, new_latents], axis=0)
    scores = jnp.einsum("thc,kc->htk", queries, key_rows, preferred_element_type=f32) * (
        VDIM + ROPE
    ) ** (-0.5)
    query_pos = jnp.arange(tok_rows, dtype=jnp.int32)[:, None]
    key_pos = jnp.arange(key_rows.shape[0], dtype=jnp.int32)[None, :] - context
    scores = jnp.where((key_pos <= query_pos)[None], scores, -jnp.inf)
    row_peak = jnp.max(scores, axis=2, keepdims=True)
    exp_scores = jnp.exp(scores - row_peak)
    attn_probs = (exp_scores / jnp.sum(exp_scores, axis=2, keepdims=True)).astype(bf16)
    return jnp.einsum(
        "htk,kl->thl", attn_probs, key_rows[:, :LATENT], preferred_element_type=f32
    ).astype(bf16)


def onehot(target, size):
    return (jnp.arange(size, dtype=jnp.int32)[:, None] == target[None, :]).astype(bf16)


def per_device(
    queries,
    latent_cache,
    new_latents,
    residual,
    w_uv,
    w_out,
    norm_gain,
    expert_ids,
    gate_weights,
    w_gate,
    w_up,
    w_down,
):
    tok_rows, head_count = queries.shape[0], queries.shape[1]
    _, width = residual.shape
    local_experts, _, ff = w_gate.shape
    experts_all = local_experts * lax.axis_size("expert")
    at = lax.axis_index("expert")
    x, y, c = at // (GY * GC), (at // GC) % GY, at % GC

    expert_row = jnp.arange(experts_all, dtype=jnp.int32)[None, :]
    dense = jnp.zeros((tok_rows, experts_all), f32)
    for k in range(expert_ids.shape[1]):
        dense = dense + jnp.where(
            expert_ids[:, k : k + 1] == expert_row, gate_weights[:, k : k + 1], 0.0
        )

    per_owner = w_out.shape[0]
    tiles = width // LANES
    small = rows_of([w_uv, dense.astype(bf16)])
    extra = -(-small.shape[0] // (tiles * 8)) * 8
    uv_rows = w_uv.shape[0]
    small = padded(small, 0, tiles * extra - small.shape[0])
    small = small.reshape(tiles, extra, LANES).transpose(1, 0, 2).reshape(extra, width)
    block = per_owner + extra
    owners = GX * GY * GC
    weights = lax.all_gather(rows_of([w_out, small]), "expert", tiled=True)
    both = together(jnp.concatenate([w_gate, w_up], axis=2))[0]

    attended = attention(queries, latent_cache, new_latents)

    small_all = weights.reshape(owners, block, width)[:, per_owner:]
    small_all = small_all.reshape(owners, extra, tiles, LANES).transpose(0, 2, 1, 3)
    small_all = small_all.reshape(owners, tiles * extra, LANES)
    uv_heads = small_all[:, :uv_rows].reshape(head_count, LATENT, VDIM)
    head_values = jnp.einsum("thl,hlv->thv", attended, uv_heads, preferred_element_type=f32)
    head_values = head_values.astype(bf16).reshape(tok_rows, head_count * VDIM)

    place_of = jnp.arange(owners * block, dtype=jnp.int32)
    column = jnp.where(
        place_of % block < per_owner, place_of // block * per_owner + place_of % block, -1
    )
    spread = jnp.dot(
        head_values, onehot(column, head_count * VDIM), preferred_element_type=f32
    ).astype(bf16)
    partial = jnp.dot(spread, weights, preferred_element_type=f32)

    gates = small_all[:, uv_rows : uv_rows + tok_rows].reshape(GX, GY, GC, tok_rows, LANES)
    gates = jnp.roll(jnp.roll(gates, -x, axis=0), -y, axis=1)
    gates = jnp.where(c == 0, gates, gates[:, :, ::-1])
    hidden_all = local_experts * ff
    chosen = onehot(
        at * local_experts + jnp.arange(hidden_all, dtype=jnp.int32) // ff, experts_all
    )
    half = tok_rows // 2

    def gate_rows(places):
        picked = []
        for i, j in places:
            for core in range(GC):
                for piece in (gates[:, i, core, :half], gates[j, :, core, half:]):
                    picked.append(piece.reshape(-1, LANES))
        return jnp.dot(rows_of(picked), chosen, preferred_element_type=f32)

    down_mat = w_down.reshape(hidden_all, width)
    partial, gates_1, gates_2, gates_3 = together(
        partial.astype(bf16),
        gate_rows([(0, 0)]),
        gate_rows([(1, 1), (3, 3)]),
        gate_rows([(2, 2)]),
    )

    own_hidden = z_scatter(partial) + residual.astype(f32)
    scale_rows = lax.rsqrt(jnp.mean(own_hidden * own_hidden, axis=1, keepdims=True) + EPSILON)
    own_normed = (own_hidden * scale_rows * norm_gain).astype(bf16)
    normed = z_gather(own_normed)

    def experts(blocks, gate_scale):
        pieces = []
        for block in blocks:
            pieces += block + [near(piece, dc=1) for piece in block]
        own, other = run_experts(pieces, gate_scale, both, down_mat, len(blocks))
        other = near(other, dc=1)
        return [[own[i], other[i]] for i in range(2 * len(blocks))]

    halves_a, halves_b = gather_direct(normed[:half], normed[half:], "dx", "dy")
    all_a, all_b = gather_pair(halves_a, halves_b, "dy", "dx")

    def block(i):
        return [*all_a[i], *all_b[i]]

    own_a, own_b = experts([block(0)], gates_1)
    after_a, after_b, before_a, before_b = experts([block(1), block(3)], gates_2)
    opposite_a, opposite_b = experts([block(2)], gates_3)
    total_a, total_b = scatter_pair(
        (own_a, after_a, opposite_a, before_a), (own_b, after_b, opposite_b, before_b), "dy", "dx"
    )
    final = scatter_direct(total_a, total_b, "dx", "dy")
    return (own_hidden + z_scatter(rows_of(final))).astype(bf16)


def solution(mesh):
    placed = (
        P("expert", "tensor", None),
        P("expert", None),
        P("expert", None),
        P(("expert", "tensor"), None),
        P(("tensor", "expert"), None),
        P(("tensor", "expert"), None),
        P(),
        P("expert", None),
        P("expert", None),
        P("expert", None, "tensor"),
        P("expert", None, "tensor"),
        P("expert", "tensor", None),
    )

    return jax.shard_map(
        per_device,
        mesh=mesh,
        in_specs=placed,
        out_specs=P(("expert", "tensor"), None),
        check_vma=False,
    )
```

```python
import jax
import jax.numpy as jnp
from jax import lax
from jax.experimental import pallas as pl
from jax.experimental.pallas import tpu as pltpu
from jax.sharding import PartitionSpec as P

GX, GY, GC = 4, 4, 2
LATENT = 512
ROPE = 64
VDIM = 128
EPSILON = 1e-06
LANES = 128


bf16 = jnp.bfloat16
f32 = jnp.float32


def place(x, y, c):
    return ((x % GX) * GY + y % GY) * GC + c % GC


def near(v, dx=0, dy=0, dc=0):
    pairs = [
        (place(x + dx, y + dy, c + dc), place(x, y, c))
        for x in range(GX)
        for y in range(GY)
        for c in range(GC)
    ]
    return lax.ppermute(v, "expert", pairs)


def together(*values):
    return lax.optimization_barrier(values)


def rows_of(parts):
    return jnp.concatenate(parts, axis=0)


def plus(*terms):
    total = terms[0].astype(f32)
    for term in terms[1:]:
        total = total + term.astype(f32)
    return total


def padded(v, above, below):
    return jnp.pad(v, ((above, below), (0, 0)))


def gather_pair(a, b, axis_a, axis_b):
    a_after, a_before = near(a[0], **{axis_a: 1}), near(a[1], **{axis_a: -1})
    b_after, b_before = near(b[0], **{axis_b: 1}), near(b[1], **{axis_b: -1})
    a_rest = near(a[1], **{axis_a: 1}), near(a[0], **{axis_a: -1})
    b_rest = near(b[1], **{axis_b: 1}), near(b[0], **{axis_b: -1})
    a_opposite = [near(a_after, **{axis_a: 1}), near(a_before, **{axis_a: -1})]
    b_opposite = [near(b_after, **{axis_b: 1}), near(b_before, **{axis_b: -1})]
    return (a, [a_after, a_rest[0]], a_opposite, [a_rest[1], a_before]), (
        b,
        [b_after, b_rest[0]],
        b_opposite,
        [b_rest[1], b_before],
    )


def gather_direct(a, b, axis_a, axis_b):
    a, b = together(a, b)
    got = [near(a, **{axis_a: k}) for k in (1, 2, -1)]
    got += [near(b, **{axis_b: k}) for k in (1, 2, -1)]
    got = together(*got)
    halves = [a, got[0]], [got[1], got[2]], [b, got[3]], [got[4], got[5]]
    halves = together(*(rows_of(half) for half in halves))
    return halves[:2], halves[2:]


def scatter_direct(a, b, axis_a, axis_b):
    size = a[0].shape[0] // 2
    blocks = [v[i * size : (i + 1) * size].astype(bf16) for v in (*a, *b) for i in range(2)]
    blocks = together(*blocks)
    sums = []
    for i, axis in ((0, axis_a), (4, axis_b)):
        got = [near(blocks[i + j], **{axis: -k}) for j, k in ((1, 1), (2, 2), (3, -1))]
        sums.append(plus(blocks[i], *got))
    return sums


def scatter_pair(a, b, axis_a, axis_b):
    half = a[0][0].shape[0] // 2

    def part(terms, second):
        cut = slice(half, None) if second else slice(0, half)
        return plus(*(term[cut] for term in terms))

    both = ((a, axis_a), (b, axis_b))
    opposite = together(*(part(v[2], i).astype(bf16) for v, _ in both for i in range(2)))
    via = [
        near(opposite[2 * n + i], **{axis: 2 * i - 1})
        for n, (_, axis) in enumerate(both)
        for i in range(2)
    ]
    plain = together(
        *(part(v[k], second).astype(bf16) for v, _ in both for k, second in ((1, 1), (3, 0)))
    )
    got = [
        near(plain[2 * n + i], **{axis: 2 * i - 1})
        for n, (_, axis) in enumerate(both)
        for i in range(2)
    ]
    merged = [
        (part(v[k], second) + via[2 * n + second].astype(f32)).astype(bf16)
        for n, (v, _) in enumerate(both)
        for k, second in ((1, 0), (3, 1))
    ]
    merged = together(*merged)
    last = [
        near(merged[2 * n + i], **{axis: 2 * i - 1})
        for n, (_, axis) in enumerate(both)
        for i in range(2)
    ]
    return [
        (
            part(v[0], 0) + plus(last[2 * n], got[2 * n + 1]),
            part(v[0], 1) + plus(got[2 * n], last[2 * n + 1]),
        )
        for n, (v, _) in enumerate(both)
    ]


def expert_kernel(*refs, blocks, count):
    pieces, (gates, both, down, own, other) = refs[:count], refs[count : count + 5]
    x, scale, active, y, x_sem, s_sem, o_sem = refs[count + 5 :]
    per_block = count // blocks
    rows, width = pieces[0].shape
    out_rows = own.shape[1]
    block_rows = per_block * rows
    local, _, ff = both.shape
    ff = ff // 2
    step = 512
    scale_copy = pltpu.make_async_copy(gates, scale, s_sem)
    x_copies = [
        pltpu.make_async_copy(
            pieces[i], x.at[i // per_block, pl.ds(i % per_block * rows, rows)], x_sem.at[i]
        )
        for i in range(count)
    ]
    for copy in x_copies[:per_block] + [scale_copy] + x_copies[per_block:]:
        copy.start()
    out_copies = []
    for b in range(blocks):
        for copy in x_copies[per_block * b : per_block * (b + 1)]:
            copy.wait()
        if b == 0:
            scale_copy.wait()
        for e in range(local):
            parts = jnp.dot(x[b], both[e], preferred_element_type=f32)
            gate_part, up_part = parts[:, :ff], parts[:, ff:]
            value = gate_part / (1.0 + jnp.exp(-gate_part)) * up_part
            value = value * scale[pl.ds(b * block_rows, block_rows), pl.ds(e * ff, ff)]
            active[:, pl.ds(e * ff, ff)] = value.astype(bf16)
        for at in range(0, width, step):
            size = min(step, width - at)
            y[b, :, pl.ds(at, size)] = jnp.dot(
                active[...], down[:, pl.ds(at, size)], preferred_element_type=f32
            ).astype(bf16)
        for i in range(4):
            copy = pltpu.make_async_copy(
                y.at[b, pl.ds(i * out_rows, out_rows)],
                (own, other)[i // 2].at[2 * b + i % 2],
                o_sem.at[4 * b + i],
            )
            copy.start()
            out_copies.append(copy)
    for copy in out_copies:
        copy.wait()


def run_experts(pieces, gates, both, down, blocks):
    count = len(pieces)
    rows, width = pieces[0].shape
    hidden = down.shape[0]
    total = count * rows
    block_rows = total // blocks
    in_hbm = pl.BlockSpec(memory_space=pltpu.HBM)
    on_chip = pl.BlockSpec(memory_space=pltpu.VMEM)
    return pl.pallas_call(
        lambda *refs: expert_kernel(*refs, blocks=blocks, count=count),
        out_shape=[jax.ShapeDtypeStruct((2 * blocks, block_rows // 4, width), bf16)] * 2,
        in_specs=[in_hbm] * (count + 1) + [on_chip] * 2,
        out_specs=[in_hbm] * 2,
        scratch_shapes=[
            pltpu.VMEM((blocks, block_rows, width), bf16),
            pltpu.VMEM((total, hidden), f32),
            pltpu.VMEM((block_rows, hidden), bf16),
            pltpu.VMEM((blocks, block_rows, width), bf16),
            pltpu.SemaphoreType.DMA((count,)),
            pltpu.SemaphoreType.DMA,
            pltpu.SemaphoreType.DMA((4 * blocks,)),
        ],
        compiler_params=pltpu.CompilerParams(vmem_limit_bytes=(12 if blocks == 1 else 20) << 20),
        cost_estimate=pl.CostEstimate(
            flops=6 * total * width * hidden,
            transcendentals=total * hidden,
            bytes_accessed=4 * total * width,
        ),
        name="experts",
    )(*pieces, gates, both, down)


def z_scatter(rows):
    parts = rows.astype(bf16).reshape(lax.axis_size("tensor"), -1, rows.shape[1])
    arrived = lax.all_to_all(parts, "tensor", split_axis=0, concat_axis=0, tiled=True)
    return arrived.astype(f32).sum(axis=0)


def z_gather(rows):
    parts = jnp.broadcast_to(rows[None], (lax.axis_size("tensor"), *rows.shape))
    arrived = lax.all_to_all(parts, "tensor", split_axis=0, concat_axis=0, tiled=True)
    return arrived.reshape(-1, rows.shape[1])


def attention(queries, latent_cache, new_latents):
    tok_rows = queries.shape[0]
    context = latent_cache.shape[0]
    key_rows = jnp.concatenate([latent_cache, new_latents], axis=0)
    scores = jnp.einsum("thc,kc->htk", queries, key_rows, preferred_element_type=f32) * (
        VDIM + ROPE
    ) ** (-0.5)
    query_pos = jnp.arange(tok_rows, dtype=jnp.int32)[:, None]
    key_pos = jnp.arange(key_rows.shape[0], dtype=jnp.int32)[None, :] - context
    scores = jnp.where((key_pos <= query_pos)[None], scores, -jnp.inf)
    row_peak = jnp.max(scores, axis=2, keepdims=True)
    exp_scores = jnp.exp(scores - row_peak)
    attn_probs = (exp_scores / jnp.sum(exp_scores, axis=2, keepdims=True)).astype(bf16)
    return jnp.einsum(
        "htk,kl->thl", attn_probs, key_rows[:, :LATENT], preferred_element_type=f32
    ).astype(bf16)


def onehot(target, size):
    return (jnp.arange(size, dtype=jnp.int32)[:, None] == target[None, :]).astype(bf16)


def per_device(
    queries,
    latent_cache,
    new_latents,
    residual,
    w_uv,
    w_out,
    norm_gain,
    expert_ids,
    gate_weights,
    w_gate,
    w_up,
    w_down,
):
    tok_rows, head_count = queries.shape[0], queries.shape[1]
    _, width = residual.shape
    local_experts, _, ff = w_gate.shape
    experts_all = local_experts * lax.axis_size("expert")
    at = lax.axis_index("expert")
    x, y, c = at // (GY * GC), (at // GC) % GY, at % GC

    expert_row = jnp.arange(experts_all, dtype=jnp.int32)[None, :]
    dense = jnp.sum(
        jnp.where(expert_ids[:, :, None] == expert_row[None], gate_weights[:, :, None], 0.0), axis=1
    )

    per_owner = w_out.shape[0]
    tiles = width // LANES
    small = rows_of([w_uv, dense.astype(bf16)])
    extra = -(-small.shape[0] // (tiles * 8)) * 8
    uv_rows = w_uv.shape[0]
    small = padded(small, 0, tiles * extra - small.shape[0])
    small = small.reshape(tiles, extra, LANES).transpose(1, 0, 2).reshape(extra, width)
    block = per_owner + extra
    owners = GX * GY * GC
    weights = lax.all_gather(rows_of([w_out, small]), "expert", tiled=True)
    both = together(jnp.concatenate([w_gate, w_up], axis=2))[0]

    attended = attention(queries, latent_cache, new_latents)

    small_all = weights.reshape(owners, block, width)[:, per_owner:]
    small_all = small_all.reshape(owners, extra, tiles, LANES).transpose(0, 2, 1, 3)
    small_all = small_all.reshape(owners, tiles * extra, LANES)
    uv_heads = small_all[:, :uv_rows].reshape(head_count, LATENT, VDIM)
    head_values = jnp.einsum("thl,hlv->thv", attended, uv_heads, preferred_element_type=f32)
    head_values = head_values.astype(bf16).reshape(tok_rows, head_count * VDIM)

    place_of = jnp.arange(owners * block, dtype=jnp.int32)
    column = jnp.where(
        place_of % block < per_owner, place_of // block * per_owner + place_of % block, -1
    )
    spread = jnp.dot(
        head_values, onehot(column, head_count * VDIM), preferred_element_type=f32
    ).astype(bf16)
    partial = jnp.dot(spread, weights, preferred_element_type=f32)

    gates = small_all[:, uv_rows : uv_rows + tok_rows].reshape(GX, GY, GC, tok_rows, LANES)
    gates = jnp.roll(jnp.roll(gates, -x, axis=0), -y, axis=1)
    gates = jnp.where(c == 0, gates, gates[:, :, ::-1])
    hidden_all = local_experts * ff
    chosen = onehot(
        at * local_experts + jnp.arange(hidden_all, dtype=jnp.int32) // ff, experts_all
    )
    half = tok_rows // 2

    def gate_rows(places):
        picked = []
        for i, j in places:
            for core in range(GC):
                for piece in (gates[:, i, core, :half], gates[j, :, core, half:]):
                    picked.append(piece.reshape(-1, LANES))
        return jnp.dot(rows_of(picked), chosen, preferred_element_type=f32)

    down_mat = w_down.reshape(hidden_all, width)
    partial, gates_1, gates_2, gates_3 = together(
        partial.astype(bf16),
        gate_rows([(0, 0)]),
        gate_rows([(1, 1), (3, 3)]),
        gate_rows([(2, 2)]),
    )

    own_hidden = z_scatter(partial) + residual.astype(f32)
    scale_rows = lax.rsqrt(jnp.mean(own_hidden * own_hidden, axis=1, keepdims=True) + EPSILON)
    own_normed = (own_hidden * scale_rows * norm_gain).astype(bf16)
    normed = z_gather(own_normed)

    def experts(blocks, gate_scale):
        pieces = []
        for block in blocks:
            pieces += block + [near(piece, dc=1) for piece in block]
        own, other = run_experts(pieces, gate_scale, both, down_mat, len(blocks))
        other = near(other, dc=1)
        return [[own[i], other[i]] for i in range(2 * len(blocks))]

    halves_a, halves_b = gather_direct(normed[:half], normed[half:], "dx", "dy")
    all_a, all_b = gather_pair(halves_a, halves_b, "dy", "dx")

    def block(i):
        return [*all_a[i], *all_b[i]]

    own_a, own_b = experts([block(0)], gates_1)
    after_a, after_b, before_a, before_b = experts([block(1), block(3)], gates_2)
    opposite_a, opposite_b = experts([block(2)], gates_3)
    total_a, total_b = scatter_pair(
        (own_a, after_a, opposite_a, before_a), (own_b, after_b, opposite_b, before_b), "dy", "dx"
    )
    final = scatter_direct(total_a, total_b, "dx", "dy")
    return (own_hidden + z_scatter(rows_of(final))).astype(bf16)


def solution(mesh):
    placed = (
        P("expert", "tensor", None),
        P("expert", None),
        P("expert", None),
        P(("expert", "tensor"), None),
        P(("tensor", "expert"), None),
        P(("tensor", "expert"), None),
        P(),
        P("expert", None),
        P("expert", None),
        P("expert", None, "tensor"),
        P("expert", None, "tensor"),
        P("expert", "tensor", None),
    )

    return jax.shard_map(
        per_device,
        mesh=mesh,
        in_specs=placed,
        out_specs=P(("expert", "tensor"), None),
        check_vma=False,
    )
```
